256 devices in a mesh: tmpl: 64 (over z_lo, y, x, core), sta: 4 (over z_hi).
Axes of the slice: x: 4, y: 4, z: 8 (z_hi: 4, z_lo: 2; z = z_hi * 2 + z_lo), core: 2. Of those that a mesh axis runs over, the one named last changes fastest.
Arguments:
- window: bfloat16 [300, 8192], P('sta', 'tmpl'), may hold values from -6 to 6
- library: bfloat16 [64, 300, 300], P(None, 'sta'), may hold values from -6 to 6
- library_index: int32 [64], P('tmpl'), may hold values from 0 to 63
- moveout: int32 [64, 300], P('tmpl', 'sta'), may hold values from 0 to 212, as said below
- group_of: int32 [300], P('sta'), may hold values from 0 to 15, never falling along the last dimension, each value on 1 to 32 neighbouring positions
Outputs:
- stacks: bfloat16 [64, 16, 7680], P('tmpl', None, 'sta')
The draws below stay inside these ranges and needn't reach their ends.
Inputs may be any that keep to these rules, and one draw needn't show every extreme that they name: Every row of moveout has some channel at 0 and some channel at 212.
All inputs are finite; a program needn't handle non-finite values.
Results may differ from the reference program's by a relative error of at most 0.01.
Values may be sent and summed in bfloat16 or wider, within the bound.
No kernel may reach another device: no remote copies, remote signals or barrier semaphores. Data moves between devices by JAX's collectives and lax.ppermute only.
A program may use at most 128 MiB of HBM per device.

```python
import math
import jax
import jax.numpy as jnp
import numpy as np
from jax import lax

CHANNELS = 300
TMPL_LEN = 300
MAX_SHIFT = 212
LIBRARY = 64
GROUPS = 16
GROUP_MOST = 32
TEMPLATES = 64
WINDOW = 8192
LAG_COUNT = 7680
N_STA = 4


def draw_moveout(key, part):
    raw = jax.random.randint(key, (TEMPLATES, CHANNELS), 0, MAX_SHIFT + 1)
    rows = jnp.arange(TEMPLATES, dtype=jnp.int32)[:, None]
    columns = jnp.arange(CHANNELS, dtype=jnp.int32)[None, :]
    lowest = columns == rows % CHANNELS
    highest = columns == (rows + 1) % CHANNELS
    shifted = jnp.where(highest, MAX_SHIFT, raw)
    return jnp.where(lowest, 0, shifted).astype(jnp.int32)


def set_ends(array, key, low, top_value):
    longest = array.shape.index(max(array.shape))
    spots = []
    for shift in (0, 1):
        where = [jax.random.randint(jax.random.fold_in(key, axis), (), 0, length) for axis, length in enumerate(array.shape)]
        where[longest] = (where[longest] + shift) % array.shape[longest]
        spots.append(tuple(where))
    return array.at[spots[0]].set(low).at[spots[1]].set(top_value)


def levels(rng, dims, cuts, smallest, top_value):
    gain = 1.0
    for dim, shards_of in cuts:
        heights = jax.random.uniform(jax.random.fold_in(jax.random.fold_in(rng, 6), dim), (shards_of,), jnp.float32, smallest / len(cuts), top_value / len(cuts))
        gain = gain * jnp.repeat(jnp.exp(heights), dims[dim] // shards_of).reshape((-1,) + (1,) * (len(dims) - 1 - dim))
    return gain


def profile(count, total, most, skew):
    portions = [(1 << 20) // math.isqrt(rank ** skew) + 1 for rank in range(2, count + 1)]
    spare, holding = total - most - (count - 1), [1] * (count - 1)
    while spare > 0:
        free = [i for i in range(count - 1) if holding[i] < most]
        mass, left = sum([portions[i] for i in free]), spare
        for i in free:
            more = min(most - holding[i], max(1, left * portions[i] // mass), spare)
            holding[i] = holding[i] + more
            spare = spare - more
    return np.array([most] + holding)


def ragged_sizes(stream_key, number_of, total, most, slope):
    if number_of == 2:
        one = jax.random.randint(stream_key, (), max(1, total - most), min(most, total - 1) + 1)
        return jnp.stack([one, total - one])
    lengths = jnp.asarray(profile(number_of, total, most, slope), jnp.int32)
    couples = (number_of - 1) // 2
    source_of, taker = lengths[1:1 + 2 * couples:2], lengths[2:2 + 2 * couples:2]
    room = jnp.minimum(source_of - 1, most - taker)
    passed = jax.random.randint(jax.random.fold_in(stream_key, 1), (couples,), 0, 1 << 20) % (room + 1)
    lengths = lengths.at[1:1 + 2 * couples:2].set(source_of - passed).at[2:2 + 2 * couples:2].set(taker + passed)
    return lengths[jax.random.permutation(jax.random.fold_in(stream_key, 2), number_of)]


def noise(rng, shape, spread, bound, cuts=(), held_as=jnp.bfloat16):
    result = spread * jax.random.normal(rng, shape, jnp.float32)
    if cuts:
        result = result * levels(rng, shape, cuts, -0.22, 0.18)
    return jnp.clip(result, -bound, bound).astype(held_as)


def setup_inputs(seed: int = 0) -> dict:
    splits = jax.random.split(jax.random.key(seed), 6)
    return {
        "window": noise(splits[0], (CHANNELS, WINDOW), 1.0, 6.0, ((0, 4), (1, 64))),
        "library": noise(splits[1], (LIBRARY, CHANNELS, TMPL_LEN), 1.0, 6.0, ((1, 4),)),
        "library_index": set_ends(jax.random.randint(splits[2], (TEMPLATES,), 0, LIBRARY), jax.random.fold_in(splits[2], 1), 0, LIBRARY - 1).astype(jnp.int32),
        "moveout": draw_moveout(jax.random.fold_in(splits[5], 71), 0),
        "group_of": jnp.searchsorted(jnp.cumsum(ragged_sizes(splits[4], GROUPS, CHANNELS, GROUP_MOST, 1)), jnp.arange(CHANNELS), side="right").astype(jnp.int32),
    }


eps = 1e-06

def normalized_templates(library, library_index):
    chosen = jnp.take(library, library_index, axis=0).astype(jnp.float32)
    centered = chosen - lax.optimization_barrier(jnp.mean(chosen, axis=-1, keepdims=True))
    factor = lax.rsqrt(lax.optimization_barrier(jnp.mean(centered * centered, axis=-1, keepdims=True)) + eps)
    return (centered * factor).astype(jnp.bfloat16)

def inverse_from_running(running):
    padded = jnp.concatenate([jnp.zeros((running.shape[0], 1), running.dtype), running], axis=1)
    mean_square = (padded[:, TMPL_LEN:] - padded[:, :-TMPL_LEN]) / TMPL_LEN
    return 1.0 / (TMPL_LEN * jnp.sqrt(mean_square + eps))

def reference(window, library, library_index, moveout, group_of):
    normalized = normalized_templates(library, library_index)
    values = window.astype(jnp.float32)
    inverse = inverse_from_running(jnp.cumsum(values * values, axis=1))
    data_freq = jnp.fft.rfft(values, axis=1)
    positions = WINDOW - TMPL_LEN + 1
    members = (group_of[:, None] == jnp.arange(GROUPS, dtype=jnp.int32)[None, :]).astype(jnp.float32)
    counts = lax.optimization_barrier(jnp.sum(members, axis=0))
    member_split = members.reshape(N_STA, CHANNELS // N_STA, GROUPS)

    def one_template(inputs):
        taps, shifts = inputs
        padded = jnp.zeros((CHANNELS, WINDOW), jnp.float32).at[:, :TMPL_LEN].set(taps.astype(jnp.float32))
        spectrum = jnp.conj(jnp.fft.rfft(padded, axis=1)) * data_freq
        full = jnp.fft.irfft(spectrum, n=WINDOW, axis=1)[:, :positions]
        weighted = full * inverse
        shifted = jax.vmap(lambda row, start: lax.dynamic_slice_in_dim(row, start, LAG_COUNT))(weighted, shifts)
        split = shifted.reshape(N_STA, CHANNELS // N_STA, LAG_COUNT)
        partial_value = jnp.einsum('scl,scg->sgl', split, member_split, precision=lax.Precision.HIGHEST)
        rounded = lax.optimization_barrier(partial_value.astype(jnp.bfloat16))
        return lax.optimization_barrier(jnp.sum(rounded.astype(jnp.float32), axis=0))
    group_sum = lax.map(one_template, (normalized, moveout))
    scale = jnp.sqrt(TMPL_LEN / counts)
    return (group_sum * scale[None, :, None]).astype(jnp.bfloat16)
```

```python
import functools

import jax
import jax.numpy as jnp
from jax import lax
from jax.experimental import pallas as pl
from jax.experimental.pallas import tpu as pltpu
from jax.sharding import PartitionSpec as P

TMPL_LEN = 300
MAX_SHIFT = 212
GROUPS = 16
CHANS = 75
LAGS = 7680
SIZES = (2, 4, 4, 2)
PITCH = 72
BUNCH = 5

eps = 1e-06


def normalized_templates(library, library_index):
    chosen = lax.dynamic_index_in_dim(library, library_index[0], 0, keepdims=False).astype(jnp.float32)
    centered = chosen - jnp.mean(chosen, axis=-1, keepdims=True)
    factor = lax.rsqrt(jnp.mean(centered * centered, axis=-1, keepdims=True) + eps)
    return (centered * factor).astype(jnp.bfloat16)


def pairs_of(move):
    z_n, y_n, x_n, c_n = SIZES

    def index(z, y, x, c):
        return ((z * y_n + y) * x_n + x) * c_n + c

    pairs = []
    for z in range(z_n):
        for y in range(y_n):
            for x in range(x_n):
                for c in range(c_n):
                    tz, ty, tx, tc = move(z, y, x, c)
                    pairs.append((index(z, y, x, c), index(tz % z_n, ty % y_n, tx % x_n, tc % c_n)))
    return pairs


def gather_window(block):
    row = [block]
    for d in (1, 2, 3):
        row.append(lax.ppermute(block, "tmpl", pairs_of(lambda z, y, x, c, d=d: (z, y, x + d, c))))
    row = jnp.stack(row)
    plane = [row]
    for dz in range(2):
        for dy in range(4):
            if dz or dy:
                move = lambda z, y, x, c, dz=dz, dy=dy: (z + dz, y + dy, x, c)
                plane.append(lax.ppermute(row, "tmpl", pairs_of(move)))
    mine = jnp.concatenate(plane)
    other = lax.ppermute(mine, "tmpl", pairs_of(lambda z, y, x, c: (z, y, x, c + 1)))
    return mine, other


def toeplitz_kernel(taps_ref, out_ref):
    def one(c, carry):
        base = jnp.broadcast_to(taps_ref[pl.ds(c, 1), :], (8, 512))
        for pair in range(8):
            halves = [
                pltpu.roll(base, 16 * pair + 8 * h, axis=1, stride=1, stride_axis=0) for h in (0, 1)
            ]
            out_ref[c, 16 * pair : 16 * pair + 16, :] = jnp.concatenate(halves, axis=0).astype(jnp.bfloat16)
        return carry

    lax.fori_loop(0, CHANS, one, 0)


def toeplitz(taps):
    padded = jnp.pad(taps.astype(jnp.float32), ((0, 0), (0, 512 - TMPL_LEN)))
    return pl.pallas_call(
        toeplitz_kernel,
        out_shape=jax.ShapeDtypeStruct((CHANS, 128, 512), jnp.bfloat16),
        in_specs=[pl.BlockSpec(memory_space=pltpu.VMEM)],
        out_specs=pl.BlockSpec(memory_space=pltpu.VMEM),
        compiler_params=pltpu.CompilerParams(vmem_limit_bytes=16 << 20),
        cost_estimate=pl.CostEstimate(flops=CHANS * 65536 * 8, bytes_accessed=CHANS * 131072, transcendentals=0),
    )(padded)


def correlate_kernel(
    place_ref, moveout_ref, group_ref, mine_ref, other_ref, band_ref, toep_ref,
    o0_ref, o1_ref, o2_ref, o3_ref, rows_ref, shift_ref, acc_ref,
):
    z0, y0, x0, c0, s0 = (place_ref[k] for k in range(5))
    first = c0 == 0
    acc_ref[...] = jnp.zeros_like(acc_ref)
    for r in (64, 65, 66):
        rows_ref[pl.ds(r, CHANS, stride=PITCH), :] = jnp.zeros((CHANS, 128), jnp.float32)
    for u in range(32):
        z, y, x = u // 16, u // 4 % 4, u % 4
        spot = (((z0 - z) & 1) * 4 + ((y0 - y) & 3)) * 4 + ((x0 - x) & 3)
        mine = mine_ref[spot].astype(jnp.float32)
        other = other_ref[spot].astype(jnp.float32)
        rows_ref[pl.ds(2 * u, CHANS, stride=PITCH), :] = jnp.where(first, mine, other)
        rows_ref[pl.ds(2 * u + 1, CHANS, stride=PITCH), :] = jnp.where(first, other, mine)

    lane = lax.broadcasted_iota(jnp.int32, (64, 128), 1)
    line = lax.broadcasted_iota(jnp.int32, (64, 128), 0)

    def bunch(step, carry):
        values, uppers, lowers = [], [], []
        for k in range(BUNCH):
            base = pl.multiple_of((step * BUNCH + k) * PITCH, 8)
            value, upper, lower = [], [], []
            for q in range(4):
                row = rows_ref[pl.ds(base + q, 64), :]
                square = row * row
                high = square.astype(jnp.bfloat16)
                value.append(row.astype(jnp.bfloat16))
                upper.append(high)
                lower.append((square - high.astype(jnp.float32)).astype(jnp.bfloat16))
            values.append(jnp.concatenate(value, axis=1))
            uppers.append(jnp.concatenate(upper, axis=1))
            lowers.append(jnp.concatenate(lower, axis=1))
        band = band_ref[...]
        form = (((1,), (0,)), ((), ()))
        total = lax.dot_general(
            jnp.concatenate(uppers, axis=0), band, form, preferred_element_type=jnp.float32
        ) + lax.dot_general(jnp.concatenate(lowers, axis=0), band, form, preferred_element_type=jnp.float32)
        inverse = lax.rsqrt(total * (1.0 / TMPL_LEN) + eps) * (1.0 / TMPL_LEN)
        for k in range(BUNCH):
            c = step * BUNCH + k
            corr = lax.dot_general(
                values[k], toep_ref[c], (((1,), (1,)), ((), ())), preferred_element_type=jnp.float32
            )
            shift_ref[k, :64, :] = corr * inverse[64 * k : 64 * k + 64]
            move = moveout_ref[c]
            skip, turn = move >> 7, move & 127
            back = (128 - turn) & 127
            low = pltpu.roll(shift_ref[k, pl.ds(skip, 64), :], back, axis=1)
            high = pltpu.roll(shift_ref[k, pl.ds(skip + 1, 64), :], back, axis=1)
            moved = jnp.where(lane < 128 - turn, low, high)
            moved = jnp.where(line < 60, moved, 1.0)
            start = pl.multiple_of(group_ref[c] * 64, 64)
            acc_ref[pl.ds(start, 64), :] += moved
        return carry

    lax.fori_loop(0, CHANS // BUNCH, bunch, 0)
    for d, out in enumerate((o0_ref, o1_ref, o2_ref, o3_ref)):
        origin = ((s0 + d) & 3) * 15
        for r in range(15):
            out[:, 128 * r : 128 * r + 128] = acc_ref[pl.ds(origin + r, GROUPS, stride=64), :].astype(jnp.bfloat16)
        out[:, 1920:2048] = acc_ref[pl.ds(60, GROUPS, stride=64), :].astype(jnp.bfloat16)


def correlate(place, moveout, group_of, mine, other, band, toep):
    smem = pl.BlockSpec(memory_space=pltpu.SMEM)
    vmem = pl.BlockSpec(memory_space=pltpu.VMEM)
    return pl.pallas_call(
        correlate_kernel,
        out_shape=[jax.ShapeDtypeStruct((GROUPS, 2048), jnp.bfloat16)] * 4,
        in_specs=[smem] * 3 + [vmem] * 4,
        out_specs=[vmem] * 4,
        scratch_shapes=[
            pltpu.VMEM((CHANS * PITCH, 128), jnp.float32),
            pltpu.VMEM((BUNCH, PITCH, 128), jnp.float32),
            pltpu.VMEM((GROUPS * 64, 128), jnp.float32),
        ],
        compiler_params=pltpu.CompilerParams(vmem_limit_bytes=32 << 20),
    )(place, moveout, group_of, mine, other, band, toep)


def window_band():
    row = lax.broadcasted_iota(jnp.int32, (512, 128), 0)
    column = lax.broadcasted_iota(jnp.int32, (512, 128), 1)
    return ((row >= column) & (row < column + TMPL_LEN)).astype(jnp.bfloat16)


def on_device(window, library, library_index, moveout, group_of):
    me = lax.axis_index("tmpl")
    place = jnp.stack([me // 32, me // 8 % 4, me // 2 % 4, me % 2, lax.axis_index("sta")]).astype(jnp.int32)
    toep = toeplitz(normalized_templates(library, library_index))
    mine, other = gather_window(window)
    parts = correlate(place, moveout[0], group_of, mine, other, window_band(), toep)
    total = parts[0].astype(jnp.float32)
    for d in (1, 2, 3):
        came = lax.ppermute(parts[d], "sta", [(i, (i + d) % 4) for i in range(4)])
        total = total + came.astype(jnp.float32)
    scale = jnp.sqrt(TMPL_LEN / total[:, 1920:1921])
    return (total[:, :1920] * scale).astype(jnp.bfloat16)[None]


def solution(mesh):
    in_specs = (P("sta", "tmpl"), P(None, "sta", None), P("tmpl"), P("tmpl", "sta"), P("sta"))
    out_specs = P("tmpl", None, "sta")
    return jax.shard_map(
        on_device, mesh=mesh, in_specs=in_specs, out_specs=out_specs, check_vma=False
    )
```

```python
import jax
import jax.numpy as jnp
from jax import lax
from jax.experimental import pallas as pl
from jax.experimental.pallas import tpu as pltpu
from jax.sharding import PartitionSpec as P

TMPL_LEN = 300
MAX_SHIFT = 212
GROUPS = 16
CHANS = 75
LAGS = 7680
SIZES = (2, 4, 4, 2)
HELD = 10
ROWS = 80
PITCH = 72
BUNCH = 25

eps = 1e-06


def normalized_templates(library, library_index):
    chosen = lax.dynamic_index_in_dim(library, library_index[0], 0, keepdims=False).astype(jnp.float32)
    centered = chosen - jnp.mean(chosen, axis=-1, keepdims=True)
    factor = lax.rsqrt(jnp.mean(centered * centered, axis=-1, keepdims=True) + eps)
    return (centered * factor).astype(jnp.bfloat16)


def pairs_of(move):
    z_n, y_n, x_n, c_n = SIZES

    def index(z, y, x, c):
        return ((z * y_n + y) * x_n + x) * c_n + c

    pairs = []
    for z in range(z_n):
        for y in range(y_n):
            for x in range(x_n):
                for c in range(c_n):
                    tz, ty, tx, tc = move(z, y, x, c)
                    pairs.append((index(z, y, x, c), index(tz % z_n, ty % y_n, tx % x_n, tc % c_n)))
    return pairs


def spread(block, moves):
    return [block] + [lax.ppermute(block, "tmpl", pairs_of(move)) for move in moves]


def join(blocks):
    return jnp.concatenate([block[None] for block in blocks])


def stack_kernel(b0_ref, b1_ref, b2_ref, b3_ref, mark_ref, out_ref):
    for k, block in enumerate((b0_ref, b1_ref, b2_ref, b3_ref)):
        out_ref[8 * k : 8 * k + 8] = block[...]


def gather_window(window, taps, meta):
    came = lax.ppermute(window, "tmpl", pairs_of(lambda z, y, x, c: (z + 1, y, x, c)))
    fill = ((0, ROWS - CHANS), (0, 0))
    part = join([jnp.pad(window, fill), jnp.pad(came, fill)])
    part = join(spread(part, [lambda z, y, x, c, d=d: (z, y, x + d, c) for d in (1, 2, 3)]))
    part, taps, meta = lax.optimization_barrier((part.reshape(8, ROWS, 128), taps, meta))
    toep, mark = toeplitz(taps, meta)
    part = spread(part, [lambda z, y, x, c, d=d: (z, y + d, x, c) for d in (1, 2, 3)])
    vmem = pl.BlockSpec(memory_space=pltpu.VMEM)
    mine = pl.pallas_call(
        stack_kernel,
        out_shape=jax.ShapeDtypeStruct((32, ROWS, 128), jnp.bfloat16),
        in_specs=[vmem] * 5,
        out_specs=vmem,
        compiler_params=pltpu.CompilerParams(vmem_limit_bytes=4 << 20),
    )(*part, mark)
    other = lax.ppermute(mine, "tmpl", pairs_of(lambda z, y, x, c: (z, y, x, c + 1)))
    return mine, other, toep, meta


def toeplitz_kernel(taps_ref, meta_ref, out_ref, mark_ref):
    mark_ref[...] = jnp.zeros_like(mark_ref)

    def several(step, carry):
        for k in range(BUNCH):
            c = step * BUNCH + k
            base = jnp.broadcast_to(taps_ref[pl.ds(c, 1), :], (8, 512))
            for pair in range(8):
                halves = [
                    pltpu.roll(base, 16 * pair + 8 * h, axis=1, stride=1, stride_axis=0) for h in (0, 1)
                ]
                both = jnp.concatenate(halves, axis=0).astype(jnp.bfloat16)
                for q in range(4):
                    b = -q % 4
                    out_ref[c, 128 * q + 16 * pair : 128 * q + 16 * pair + 16, :] = both[:, 128 * b : 128 * b + 128]
        return carry

    lax.fori_loop(0, CHANS // BUNCH, several, 0)


def toeplitz(taps, meta):
    row = lax.broadcasted_iota(jnp.int32, (TMPL_LEN, 512), 0)
    column = lax.broadcasted_iota(jnp.int32, (TMPL_LEN, 512), 1)
    turned = jnp.dot(taps, (((row + column) & 511) == 0).astype(jnp.bfloat16), preferred_element_type=jnp.float32)
    return pl.pallas_call(
        toeplitz_kernel,
        out_shape=[
            jax.ShapeDtypeStruct((CHANS, 512, 128), jnp.bfloat16),
            jax.ShapeDtypeStruct((8, 128), jnp.float32),
        ],
        in_specs=[pl.BlockSpec(memory_space=pltpu.VMEM), pl.BlockSpec(memory_space=pl.ANY)],
        out_specs=[pl.BlockSpec(memory_space=pltpu.VMEM)] * 2,
        compiler_params=pltpu.CompilerParams(vmem_limit_bytes=16 << 20),
        cost_estimate=pl.CostEstimate(flops=CHANS * 65536 * 8, bytes_accessed=CHANS * 131072, transcendentals=0),
    )(turned, meta)


def correlate_kernel(
    meta_ref, mine_ref, other_ref, toep_ref,
    o0_ref, o1_ref, o2_ref, o3_ref, rows_ref, inverse_ref, square_ref, shift_ref, acc_ref, band_ref,
):
    z0, y0, x0, c0, s0 = (meta_ref[k] for k in range(5))
    first = c0 == 0
    acc_ref[...] = jnp.zeros_like(acc_ref)
    band_ref[...] = window_band()
    for r in (64, 65, 66):
        rows_ref[pl.ds(r, CHANS, stride=PITCH), :] = jnp.zeros((CHANS, 128), jnp.float32)
        square_ref[r * ROWS : (r + 1) * ROWS, :] = jnp.zeros((ROWS, 128), jnp.bfloat16)
    for u in range(32):
        z, y, x = u // 16, u // 4 % 4, u % 4
        spot = (((y0 - y) & 3) * 4 + ((x0 - x) & 3)) * 2 + ((z0 - z) & 1)
        mine = mine_ref[spot].astype(jnp.float32)
        other = other_ref[spot].astype(jnp.float32)
        for i, block in ((2 * u, jnp.where(first, mine, other)), (2 * u + 1, jnp.where(first, other, mine))):
            rows_ref[pl.ds(i, CHANS, stride=PITCH), :] = block[:CHANS]
            square_ref[i * ROWS : (i + 1) * ROWS, :] = (block * block).astype(jnp.bfloat16)

    for part in range(8):
        squares = jnp.concatenate(
            [square_ref[(8 * part + q) * ROWS : (8 * part + q + 8) * ROWS, :] for q in range(4)], axis=1
        )
        total = lax.dot_general(
            squares, band_ref[...], (((1,), (0,)), ((), ())), preferred_element_type=jnp.float32
        )
        inverse = lax.rsqrt(total * (1.0 / TMPL_LEN) + eps) * (1.0 / TMPL_LEN)
        for k in range(8):
            inverse_ref[pl.ds(8 * part + k, CHANS, stride=PITCH), :] = inverse[k * ROWS : k * ROWS + CHANS]

    lane = lax.broadcasted_iota(jnp.int32, (64, 128), 1)
    line = lax.broadcasted_iota(jnp.int32, (64, 128), 0)

    def bunch(step, carry):
        for k in range(BUNCH):
            c = step * BUNCH + k
            base = pl.multiple_of(c * PITCH, 8)
            values = jnp.concatenate(
                [rows_ref[pl.ds(base + q, 64), :].astype(jnp.bfloat16) for q in range(4)], axis=1
            )
            corr = lax.dot_general(
                values, toep_ref[c], (((1,), (0,)), ((), ())), preferred_element_type=jnp.float32
            )
            shift_ref[k, :64, :] = corr * inverse_ref[pl.ds(base, 64), :]
            move = meta_ref[5 + c]
            skip, turn = move >> 7, move & 127
            back = (128 - turn) & 127
            low = pltpu.roll(shift_ref[k, pl.ds(skip, 64), :], back, axis=1)
            high = pltpu.roll(shift_ref[k, pl.ds(skip + 1, 64), :], back, axis=1)
            moved = jnp.where(lane < 128 - turn, low, high)
            moved = jnp.where(line < 60, moved, 1.0)
            start = pl.multiple_of((meta_ref[5 + CHANS + c] - 2 * s0) * 64, 64)
            acc_ref[pl.ds(start, 64), :] += moved
        return carry

    lax.fori_loop(0, CHANS // BUNCH, bunch, 0)
    last = lax.broadcasted_iota(jnp.int32, (8, 128), 0) == 7
    for d, out in enumerate((o0_ref, o1_ref, o2_ref, o3_ref)):
        origin = ((s0 + d) & 3) * 15
        for g in range(HELD):
            upper = acc_ref[pl.ds(64 * g + origin, 8), :]
            lower = acc_ref[pl.ds(64 * g + origin + 8, 8), :]
            lower = jnp.where(last, acc_ref[64 * g + 56 : 64 * g + 64, :], lower)
            out[16 * g : 16 * g + 16, :] = jnp.concatenate([upper, lower], axis=0).astype(jnp.bfloat16)


def combine_kernel(meta_ref, p0_ref, p1_ref, p2_ref, p3_ref, out_ref, sum_ref):
    s0 = meta_ref[4]
    sum_ref[...] = jnp.zeros_like(sum_ref)
    for d, part in enumerate((p0_ref, p1_ref, p2_ref, p3_ref)):
        start = pl.multiple_of(((s0 - d) & 3) * 32, 32)
        sum_ref[pl.ds(start, HELD * 16), :] += part[...].astype(jnp.float32)
    scale = jnp.sqrt(TMPL_LEN / sum_ref[pl.ds(15, GROUPS, stride=16), :])
    for r in range(15):
        rows = sum_ref[pl.ds(r, GROUPS, stride=16), :]
        out_ref[:, 128 * r : 128 * r + 128] = (rows * scale).astype(jnp.bfloat16)


def combine(meta, parts):
    vmem = pl.BlockSpec(memory_space=pltpu.VMEM)
    return pl.pallas_call(
        combine_kernel,
        out_shape=jax.ShapeDtypeStruct((GROUPS, 1920), jnp.bfloat16),
        in_specs=[pl.BlockSpec(memory_space=pltpu.SMEM)] + [vmem] * 4,
        out_specs=vmem,
        scratch_shapes=[pltpu.VMEM((256, 128), jnp.float32)],
        compiler_params=pltpu.CompilerParams(vmem_limit_bytes=4 << 20),
    )(meta, *parts)


def correlate(meta, mine, other, toep):
    smem = pl.BlockSpec(memory_space=pltpu.SMEM)
    vmem = pl.BlockSpec(memory_space=pltpu.VMEM)
    return pl.pallas_call(
        correlate_kernel,
        out_shape=[jax.ShapeDtypeStruct((HELD * 16, 128), jnp.bfloat16)] * 4,
        in_specs=[smem] + [vmem] * 3,
        out_specs=[vmem] * 4,
        scratch_shapes=[
            pltpu.VMEM((CHANS * PITCH, 128), jnp.float32),
            pltpu.VMEM((CHANS * PITCH, 128), jnp.float32),
            pltpu.VMEM((67 * ROWS, 128), jnp.bfloat16),
            pltpu.VMEM((BUNCH, PITCH, 128), jnp.float32),
            pltpu.VMEM((HELD * 64, 128), jnp.float32),
            pltpu.VMEM((512, 128), jnp.bfloat16),
        ],
        compiler_params=pltpu.CompilerParams(vmem_limit_bytes=32 << 20),
    )(meta, mine, other, toep)


def window_band():
    row = lax.broadcasted_iota(jnp.int32, (512, 128), 0)
    column = lax.broadcasted_iota(jnp.int32, (512, 128), 1)
    return jnp.where((row >= column) & (row < column + TMPL_LEN), 1.0, 0.0).astype(jnp.bfloat16)


def on_device(window, library, library_index, moveout, group_of):
    me = lax.axis_index("tmpl")
    place = jnp.stack([me >> 5, (me >> 3) & 3, (me >> 1) & 3, me & 1, lax.axis_index("sta")]).astype(jnp.int32)
    meta = jnp.concatenate([place, moveout[0], group_of])
    mine, other, toep, meta = gather_window(window, normalized_templates(library, library_index), meta)
    parts = correlate(meta, mine, other, toep)
    came = [parts[0]]
    for d in (1, 2, 3):
        came.append(lax.ppermute(parts[d], "sta", [(i, (i + d) % 4) for i in range(4)]))
    return combine(meta, came)[None]


def solution(mesh):
    in_specs = (P("sta", "tmpl"), P(None, "sta", None), P("tmpl"), P("tmpl", "sta"), P("sta"))
    out_specs = P("tmpl", None, "sta")
    return jax.shard_map(
        on_device, mesh=mesh, in_specs=in_specs, out_specs=out_specs, check_vma=False
    )
```

```python
import jax
import jax.numpy as jnp
from jax import lax
from jax.experimental import pallas as pl
from jax.experimental.pallas import tpu as pltpu
from jax.sharding import PartitionSpec as P


TMPL_LEN = 300
GROUPS = 16
CHANS = 75
SIZES = (2, 4, 4, 2)
HELD = 10
ROWS = 80
PITCH = 72
BUNCH = 25

eps = 1e-06


def normalized_templates(library, library_index):
    chosen = lax.dynamic_index_in_dim(library, library_index[0], 0, keepdims=False).astype(jnp.float32)
    centered = chosen - jnp.mean(chosen, axis=-1, keepdims=True)
    factor = lax.rsqrt(jnp.mean(centered * centered, axis=-1, keepdims=True) + eps)
    return (centered * factor).astype(jnp.bfloat16)


def pairs_of(move):
    z_n, y_n, x_n, c_n = SIZES

    def index(z, y, x, c):
        return ((z * y_n + y) * x_n + x) * c_n + c

    pairs = []
    for z in range(z_n):
        for y in range(y_n):
            for x in range(x_n):
                for c in range(c_n):
                    tz, ty, tx, tc = move(z, y, x, c)
                    pairs.append((index(z, y, x, c), index(tz % z_n, ty % y_n, tx % x_n, tc % c_n)))
    return pairs


def spread(block, moves):
    came = [block]
    for move in moves:
        came.append(lax.ppermute(block, "tmpl", pairs_of(move)))
    return came


def join(blocks):
    return jnp.concatenate([block[None] for block in blocks])


def gather_window(window, taps, meta):
    came = lax.ppermute(window, "tmpl", pairs_of(lambda z, y, x, c: (z + 1, y, x, c)))
    fill = ((0, ROWS - CHANS), (0, 0))
    part = join([jnp.pad(window, fill), jnp.pad(came, fill)])
    part = join(spread(part, [lambda z, y, x, c, d=d: (z, y, x + d, c) for d in (1, 2, 3)]))
    part, taps, meta = lax.optimization_barrier((part.reshape(8, ROWS, 128), taps, meta))
    toep = toeplitz(taps, meta)
    part = spread(part, [lambda z, y, x, c, d=d: (z, y + d, x, c) for d in (1, 2, 3)])
    other = []
    for piece in part:
        other.append(lax.ppermute(piece, "tmpl", pairs_of(lambda z, y, x, c: (z, y, x, c + 1))))
    return part + other, toep, meta


def toeplitz_kernel(taps_ref, meta_ref, out_ref):
    def several(step, carry):
        for k in range(BUNCH):
            c = step * BUNCH + k
            base = jnp.broadcast_to(taps_ref[pl.ds(c, 1), :], (8, 512))
            for pair in range(8):
                halves = [
                    pltpu.roll(base, 16 * pair + 8 * h, axis=1, stride=1, stride_axis=0) for h in (0, 1)
                ]
                both = jnp.concatenate(halves, axis=0).astype(jnp.bfloat16)
                for q in range(4):
                    b = -q % 4
                    out_ref[c, 128 * q + 16 * pair : 128 * q + 16 * pair + 16, :] = both[:, 128 * b : 128 * b + 128]
        return carry

    lax.fori_loop(0, CHANS // BUNCH, several, 0)


def toeplitz(taps, meta):
    row = lax.broadcasted_iota(jnp.int32, (TMPL_LEN, 512), 0)
    column = lax.broadcasted_iota(jnp.int32, (TMPL_LEN, 512), 1)
    turned = jnp.dot(taps, (((row + column) & 511) == 0).astype(jnp.bfloat16), preferred_element_type=jnp.float32)
    return pl.pallas_call(
        toeplitz_kernel,
        out_shape=jax.ShapeDtypeStruct((CHANS, 512, 128), jnp.bfloat16),
        in_specs=[pl.BlockSpec(memory_space=pltpu.VMEM), pl.BlockSpec(memory_space=pl.ANY)],
        out_specs=pl.BlockSpec(memory_space=pltpu.VMEM),
        compiler_params=pltpu.CompilerParams(vmem_limit_bytes=16 << 20),
        cost_estimate=pl.CostEstimate(flops=CHANS * 65536 * 8, bytes_accessed=CHANS * 131072, transcendentals=0),
    )(turned, meta)


def correlate_kernel(
    meta_ref, m0_ref, m1_ref, m2_ref, m3_ref, n0_ref, n1_ref, n2_ref, n3_ref, toep_ref,
    o0_ref, o1_ref, o2_ref, o3_ref, rows_ref, inverse_ref, square_ref, shift_ref, acc_ref, band_ref,
):
    z0, y0, x0, c0, s0 = (meta_ref[k] for k in range(5))
    acc_ref[...] = jnp.zeros_like(acc_ref)
    band_ref[...] = window_band()
    square_ref[64 * ROWS : 65 * ROWS, :] = jnp.zeros((ROWS, 128), jnp.bfloat16)
    for r in (64, 65, 66):
        rows_ref[pl.ds(r, CHANS, stride=PITCH), :] = jnp.zeros((CHANS, 128), jnp.float32)
    pieces = ((m0_ref, n0_ref), (m1_ref, n1_ref), (m2_ref, n2_ref), (m3_ref, n3_ref))
    for dy, both in enumerate(pieces):
        for dx in range(4):
            for dz in range(2):
                spot = ((((z0 - dz) & 1) * 4 + ((y0 - dy) & 3)) * 4 + ((x0 - dx) & 3)) * 2
                for piece, i in zip(both, (spot + c0, spot + 1 - c0)):
                    block = piece[2 * dx + dz].astype(jnp.float32)
                    rows_ref[pl.ds(i, CHANS, stride=PITCH), :] = block[:CHANS]
                    square_ref[pl.ds(pl.multiple_of(i * ROWS, 16), ROWS), :] = (block * block).astype(jnp.bfloat16)

    carried = jnp.zeros((2 * ROWS, 128), jnp.float32)
    for part in reversed(range(8)):
        squares = jnp.concatenate(
            [square_ref[(8 * part + q) * ROWS : (8 * part + q + 8) * ROWS, :] for q in range(2)], axis=1
        )
        sums = lax.dot_general(
            squares, band_ref[...], (((1,), (0,)), ((), ())), preferred_element_type=jnp.float32
        )
        later = sums[:, 128:]
        total = sums[:, :128] + jnp.concatenate([later[2 * ROWS :], carried], axis=0)
        carried = later[: 2 * ROWS]
        inverse = lax.rsqrt(total * (1.0 / TMPL_LEN) + eps) * (1.0 / TMPL_LEN)
        for k in range(8):
            inverse_ref[pl.ds(8 * part + k, CHANS, stride=PITCH), :] = inverse[k * ROWS : k * ROWS + CHANS]

    lane = lax.broadcasted_iota(jnp.int32, (64, 128), 1)
    line = lax.broadcasted_iota(jnp.int32, (64, 128), 0)

    def bunch(step, carry):
        for k in range(BUNCH):
            c = step * BUNCH + k
            base = pl.multiple_of(c * PITCH, 8)
            values = jnp.concatenate(
                [rows_ref[pl.ds(base + q, 64), :].astype(jnp.bfloat16) for q in range(4)], axis=1
            )
            corr = lax.dot_general(
                values, toep_ref[c], (((1,), (0,)), ((), ())), preferred_element_type=jnp.float32
            )
            shift_ref[k, :64, :] = corr * inverse_ref[pl.ds(base, 64), :]
            move = meta_ref[5 + c]
            skip, turn = move >> 7, move & 127
            back = (128 - turn) & 127
            low = pltpu.roll(shift_ref[k, pl.ds(skip, 64), :], back, axis=1)
            high = pltpu.roll(shift_ref[k, pl.ds(skip + 1, 64), :], back, axis=1)
            moved = jnp.where(lane < 128 - turn, low, high)
            moved = jnp.where(line < 60, moved, 1.0)
            start = pl.multiple_of((meta_ref[5 + CHANS + c] - 2 * s0) * 64, 64)
            acc_ref[pl.ds(start, 64), :] += moved
        return carry

    lax.fori_loop(0, CHANS // BUNCH, bunch, 0)
    last = lax.broadcasted_iota(jnp.int32, (8, 128), 0) == 7
    for d, out in enumerate((o0_ref, o1_ref, o2_ref, o3_ref)):
        origin = ((s0 + d) & 3) * 15
        for g in range(HELD):
            upper = acc_ref[pl.ds(64 * g + origin, 8), :]
            lower = acc_ref[pl.ds(64 * g + origin + 8, 8), :]
            lower = jnp.where(last, acc_ref[64 * g + 56 : 64 * g + 64, :], lower)
            out[16 * g : 16 * g + 16, :] = jnp.concatenate([upper, lower], axis=0).astype(jnp.bfloat16)


def combine_kernel(p0_ref, p1_ref, p2_ref, p3_ref, out_ref, sum_ref):
    s0 = lax.axis_index("sta")
    sum_ref[...] = jnp.zeros_like(sum_ref)
    for d, part in enumerate((p0_ref, p1_ref, p2_ref, p3_ref)):
        start = pl.multiple_of(((s0 - d) & 3) * 32, 32)
        sum_ref[pl.ds(start, HELD * 16), :] += part[...].astype(jnp.float32)
    scale = jnp.sqrt(TMPL_LEN / sum_ref[pl.ds(15, GROUPS, stride=16), :])
    for r in range(15):
        rows = sum_ref[pl.ds(r, GROUPS, stride=16), :]
        out_ref[:, 128 * r : 128 * r + 128] = (rows * scale).astype(jnp.bfloat16)


def combine(parts):
    vmem = pl.BlockSpec(memory_space=pltpu.VMEM)
    return pl.pallas_call(
        combine_kernel,
        out_shape=jax.ShapeDtypeStruct((GROUPS, 1920), jnp.bfloat16),
        in_specs=[vmem] * 4,
        out_specs=vmem,
        scratch_shapes=[pltpu.VMEM((256, 128), jnp.float32)],
        compiler_params=pltpu.CompilerParams(vmem_limit_bytes=4 << 20),
    )(*parts)


def correlate(meta, pieces, toep):
    smem = pl.BlockSpec(memory_space=pltpu.SMEM)
    vmem = pl.BlockSpec(memory_space=pltpu.VMEM)
    return pl.pallas_call(
        correlate_kernel,
        out_shape=[jax.ShapeDtypeStruct((HELD * 16, 128), jnp.bfloat16)] * 4,
        in_specs=[smem] + [vmem] * 9,
        out_specs=[vmem] * 4,
        scratch_shapes=[
            pltpu.VMEM((CHANS * PITCH, 128), jnp.float32),
            pltpu.VMEM((CHANS * PITCH, 128), jnp.float32),
            pltpu.VMEM((65 * ROWS, 128), jnp.bfloat16),
            pltpu.VMEM((BUNCH, PITCH, 128), jnp.float32),
            pltpu.VMEM((HELD * 64, 128), jnp.float32),
            pltpu.VMEM((256, 256), jnp.bfloat16),
        ],
        compiler_params=pltpu.CompilerParams(vmem_limit_bytes=32 << 20),
    )(meta, *pieces, toep)


def window_band():
    column = lax.broadcasted_iota(jnp.int32, (256, 256), 1)
    late = column >= 128
    row = lax.broadcasted_iota(jnp.int32, (256, 256), 0) + jnp.where(late, 256, 0)
    first = column - jnp.where(late, 128, 0)
    return jnp.where((row >= first) & (row < first + TMPL_LEN), 1.0, 0.0).astype(jnp.bfloat16)


def on_device(window, library, library_index, moveout, group_of):
    me = lax.axis_index("tmpl")
    taps = normalized_templates(library, library_index)
    place = jnp.stack([me >> 5, (me >> 3) & 3, (me >> 1) & 3, me & 1, lax.axis_index("sta")]).astype(jnp.int32)
    meta = jnp.concatenate([place, moveout[0], group_of])
    pieces, toep, meta = gather_window(window, taps, meta)
    parts = correlate(meta, pieces, toep)
    came = [parts[0]]
    for d in (1, 2, 3):
        came.append(lax.ppermute(parts[d], "sta", [(i, (i + d) % 4) for i in range(4)]))
    return combine(came)[None]


def solution(mesh):
    in_specs = (P("sta", "tmpl"), P(None, "sta", None), P("tmpl"), P("tmpl", "sta"), P("sta"))
    out_specs = P("tmpl", None, "sta")

    return jax.shard_map(on_device, mesh=mesh, in_specs=in_specs, out_specs=out_specs, check_vma=False)
```

```python
import jax
import jax.numpy as jnp
from jax import lax
from jax.experimental import pallas as pl
from jax.experimental.pallas import tpu as pltpu
from jax.sharding import PartitionSpec as P


TMPL_LEN = 300
GROUPS = 16
CHANS = 75
SIZES = (2, 4, 4, 2)
HELD = 10
ROWS = 80
PITCH = 72
BUNCH = 25

eps = 1e-06


def normalized_templates(library, library_index):
    chosen = lax.dynamic_index_in_dim(library, library_index[0], 0, keepdims=False).astype(jnp.float32)
    centered = chosen - jnp.mean(chosen, axis=-1, keepdims=True)
    factor = lax.rsqrt(jnp.mean(centered * centered, axis=-1, keepdims=True) + eps)
    return (centered * factor).astype(jnp.bfloat16)


def pairs_of(move):
    z_n, y_n, x_n, c_n = SIZES

    def index(z, y, x, c):
        return ((z * y_n + y) * x_n + x) * c_n + c

    pairs = []
    for z in range(z_n):
        for y in range(y_n):
            for x in range(x_n):
                for c in range(c_n):
                    tz, ty, tx, tc = move(z, y, x, c)
                    pairs.append((index(z, y, x, c), index(tz % z_n, ty % y_n, tx % x_n, tc % c_n)))
    return pairs


def spread(block, moves):
    came = [block]
    for move in moves:
        came.append(lax.ppermute(block, "tmpl", pairs_of(move)))
    return came


def join(blocks):
    return jnp.concatenate([block[None] for block in blocks])


def gather_window(window, taps, meta):
    came = lax.ppermute(window, "tmpl", pairs_of(lambda z, y, x, c: (z + 1, y, x, c)))
    fill = ((0, ROWS - CHANS), (0, 0))
    part = join([jnp.pad(window, fill), jnp.pad(came, fill)])
    part = join(spread(part, [lambda z, y, x, c, d=d: (z, y, x + d, c) for d in (1, 2, 3)]))
    part, taps, meta = lax.optimization_barrier((part.reshape(8, ROWS, 128), taps, meta))
    toep = toeplitz(taps, meta)
    part = spread(part, [lambda z, y, x, c, d=d: (z, y + d, x, c) for d in (1, 2, 3)])
    other = []
    for piece in part:
        other.append(lax.ppermute(piece, "tmpl", pairs_of(lambda z, y, x, c: (z, y, x, c + 1))))
    return part + other, toep, meta


def toeplitz_kernel(taps_ref, meta_ref, out_ref):
    def several(step, carry):
        for k in range(BUNCH):
            c = step * BUNCH + k
            base = jnp.broadcast_to(taps_ref[pl.ds(c, 1), :], (8, 512))
            for pair in range(8):
                halves = [
                    pltpu.roll(base, 16 * pair + 8 * h, axis=1, stride=1, stride_axis=0) for h in (0, 1)
                ]
                both = jnp.concatenate(halves, axis=0).astype(jnp.bfloat16)
                for q in range(4):
                    b = -q % 4
                    out_ref[c, 16 * pair : 16 * pair + 16, 128 * q : 128 * q + 128] = both[:, 128 * b : 128 * b + 128]
        return carry

    lax.fori_loop(0, CHANS // BUNCH, several, 0)


def toeplitz(taps, meta):
    row = lax.broadcasted_iota(jnp.int32, (TMPL_LEN, 512), 0)
    column = lax.broadcasted_iota(jnp.int32, (TMPL_LEN, 512), 1)
    turned = jnp.dot(taps, (((row + column) & 511) == 0).astype(jnp.bfloat16), preferred_element_type=jnp.float32)
    return pl.pallas_call(
        toeplitz_kernel,
        out_shape=jax.ShapeDtypeStruct((CHANS, 128, 512), jnp.bfloat16),
        in_specs=[pl.BlockSpec(memory_space=pltpu.VMEM), pl.BlockSpec(memory_space=pl.ANY)],
        out_specs=pl.BlockSpec(memory_space=pltpu.VMEM),
        compiler_params=pltpu.CompilerParams(vmem_limit_bytes=16 << 20),
        cost_estimate=pl.CostEstimate(flops=CHANS * 65536 * 8, bytes_accessed=CHANS * 131072, transcendentals=0),
    )(turned, meta)


def correlate_kernel(
    meta_ref, m0_ref, m1_ref, m2_ref, m3_ref, n0_ref, n1_ref, n2_ref, n3_ref, toep_ref,
    o0_ref, o1_ref, o2_ref, o3_ref, rows_ref, inverse_ref, square_ref, shift_ref, acc_ref, band_ref, later_ref,
):
    z0, y0, x0, c0, s0 = (meta_ref[k] for k in range(5))
    acc_ref[...] = jnp.zeros_like(acc_ref)
    band_ref[...] = window_band()
    later_ref[:, 64:, :] = jnp.zeros((3 * BUNCH, PITCH - 64, 128), jnp.float32)
    square_ref[64 * ROWS : 65 * ROWS, :] = jnp.zeros((ROWS, 128), jnp.bfloat16)
    pieces = ((m0_ref, n0_ref), (m1_ref, n1_ref), (m2_ref, n2_ref), (m3_ref, n3_ref))
    for dy, both in enumerate(pieces):
        for dx in range(4):
            for dz in range(2):
                spot = ((((z0 - dz) & 1) * 4 + ((y0 - dy) & 3)) * 4 + ((x0 - dx) & 3)) * 2
                for piece, i in zip(both, (spot + c0, spot + 1 - c0)):
                    block = piece[2 * dx + dz].astype(jnp.float32)
                    rows_ref[pl.ds(i, CHANS, stride=PITCH), :] = block[:CHANS]
                    square_ref[pl.ds(pl.multiple_of(i * ROWS, 16), ROWS), :] = (block * block).astype(jnp.bfloat16)

    carried = jnp.zeros((2 * ROWS, 128), jnp.float32)
    for part in reversed(range(8)):
        squares = jnp.concatenate(
            [square_ref[(8 * part + q) * ROWS : (8 * part + q + 8) * ROWS, :] for q in range(2)], axis=1
        )
        sums = lax.dot_general(
            squares, band_ref[...], (((1,), (0,)), ((), ())), preferred_element_type=jnp.float32
        )
        later = sums[:, 128:]
        total = sums[:, :128] + jnp.concatenate([later[2 * ROWS :], carried], axis=0)
        carried = later[: 2 * ROWS]
        inverse = lax.rsqrt(total * (1.0 / TMPL_LEN) + eps) * (1.0 / TMPL_LEN)
        for k in range(8):
            inverse_ref[pl.ds(8 * part + k, CHANS, stride=PITCH), :] = inverse[k * ROWS : k * ROWS + CHANS]

    lane = lax.broadcasted_iota(jnp.int32, (64, 128), 1)
    line = lax.broadcasted_iota(jnp.int32, (64, 128), 0)

    def bunch(step, carry):
        for k in range(BUNCH):
            c = step * BUNCH + k
            base = pl.multiple_of(c * PITCH, 8)
            parts = lax.dot_general(
                rows_ref[pl.ds(base, 64), :].astype(jnp.bfloat16),
                toep_ref[c],
                (((1,), (0,)), ((), ())),
                preferred_element_type=jnp.float32,
            )
            corr = parts[:, :128]
            for q in (1, 2, 3):
                later_ref[3 * k + q - 1, :64, :] = parts[:, 128 * q : 128 * q + 128]
            for q in (1, 2, 3):
                corr = corr + later_ref[3 * k + q - 1, q : q + 64, :]
            move = meta_ref[5 + c]
            skip, turn = move >> 7, move & 127
            back = (128 - turn) & 127
            shift_ref[k, :64, :] = pltpu.roll(corr * inverse_ref[pl.ds(base, 64), :], back, axis=1)
            moved = jnp.where(
                lane < 128 - turn, shift_ref[k, pl.ds(skip, 64), :], shift_ref[k, pl.ds(skip + 1, 64), :]
            )
            moved = jnp.where(line < 60, moved, 1.0)
            start = pl.multiple_of((meta_ref[5 + CHANS + c] - 2 * s0) * 64, 64)
            acc_ref[pl.ds(start, 64), :] += moved
        return carry

    lax.fori_loop(0, CHANS // BUNCH, bunch, 0)
    last = lax.broadcasted_iota(jnp.int32, (8, 128), 0) == 7
    for d, out in enumerate((o0_ref, o1_ref, o2_ref, o3_ref)):
        origin = ((s0 + d) & 3) * 15
        for g in range(HELD):
            upper = acc_ref[pl.ds(64 * g + origin, 8), :]
            lower = acc_ref[pl.ds(64 * g + origin + 8, 8), :]
            lower = jnp.where(last, acc_ref[64 * g + 56 : 64 * g + 64, :], lower)
            out[16 * g : 16 * g + 16, :] = jnp.concatenate([upper, lower], axis=0).astype(jnp.bfloat16)


def combine_kernel(p0_ref, p1_ref, p2_ref, p3_ref, out_ref, sum_ref):
    s0 = lax.axis_index("sta")
    sum_ref[...] = jnp.zeros_like(sum_ref)
    for d, part in enumerate((p0_ref, p1_ref, p2_ref, p3_ref)):
        start = pl.multiple_of(((s0 - d) & 3) * 32, 32)
        sum_ref[pl.ds(start, HELD * 16), :] += part[...].astype(jnp.float32)
    scale = jnp.sqrt(TMPL_LEN / sum_ref[pl.ds(15, GROUPS, stride=16), :])
    for r in range(15):
        rows = sum_ref[pl.ds(r, GROUPS, stride=16), :]
        out_ref[:, 128 * r : 128 * r + 128] = (rows * scale).astype(jnp.bfloat16)


def combine(parts):
    vmem = pl.BlockSpec(memory_space=pltpu.VMEM)
    return pl.pallas_call(
        combine_kernel,
        out_shape=jax.ShapeDtypeStruct((GROUPS, 1920), jnp.bfloat16),
        in_specs=[vmem] * 4,
        out_specs=vmem,
        scratch_shapes=[pltpu.VMEM((256, 128), jnp.float32)],
        compiler_params=pltpu.CompilerParams(vmem_limit_bytes=4 << 20),
    )(*parts)


def correlate(meta, pieces, toep):
    smem = pl.BlockSpec(memory_space=pltpu.SMEM)
    vmem = pl.BlockSpec(memory_space=pltpu.VMEM)
    return pl.pallas_call(
        correlate_kernel,
        out_shape=[jax.ShapeDtypeStruct((HELD * 16, 128), jnp.bfloat16)] * 4,
        in_specs=[smem] + [vmem] * 9,
        out_specs=[vmem] * 4,
        scratch_shapes=[
            pltpu.VMEM((CHANS * PITCH, 128), jnp.float32),
            pltpu.VMEM((CHANS * PITCH, 128), jnp.float32),
            pltpu.VMEM((65 * ROWS, 128), jnp.bfloat16),
            pltpu.VMEM((BUNCH, PITCH, 128), jnp.float32),
            pltpu.VMEM((HELD * 64, 128), jnp.float32),
            pltpu.VMEM((256, 256), jnp.bfloat16),
            pltpu.VMEM((3 * BUNCH, PITCH, 128), jnp.float32),
        ],
        compiler_params=pltpu.CompilerParams(vmem_limit_bytes=32 << 20),
    )(meta, *pieces, toep)


def window_band():
    column = lax.broadcasted_iota(jnp.int32, (256, 256), 1)
    late = column >= 128
    row = lax.broadcasted_iota(jnp.int32, (256, 256), 0) + jnp.where(late, 256, 0)
    first = column - jnp.where(late, 128, 0)
    return jnp.where((row >= first) & (row < first + TMPL_LEN), 1.0, 0.0).astype(jnp.bfloat16)


def on_device(window, library, library_index, moveout, group_of):
    me = lax.axis_index("tmpl")
    taps = normalized_templates(library, library_index)
    place = jnp.stack([me >> 5, (me >> 3) & 3, (me >> 1) & 3, me & 1, lax.axis_index("sta")]).astype(jnp.int32)
    meta = jnp.concatenate([place, moveout[0], group_of])
    pieces, toep, meta = gather_window(window, taps, meta)
    parts = correlate(meta, pieces, toep)
    came = [parts[0]]
    for d in (1, 2, 3):
        came.append(lax.ppermute(parts[d], "sta", [(i, (i + d) % 4) for i in range(4)]))
    return combine(came)[None]


def solution(mesh):
    in_specs = (P("sta", "tmpl"), P(None, "sta", None), P("tmpl"), P("tmpl", "sta"), P("sta"))
    out_specs = P("tmpl", None, "sta")

    return jax.shard_map(on_device, mesh=mesh, in_specs=in_specs, out_specs=out_specs, check_vma=False)
```

```python
import functools

import jax
import jax.numpy as jnp
from jax import lax
from jax.experimental import pallas as pl
from jax.experimental.pallas import tpu as pltpu
from jax.sharding import PartitionSpec as P


TMPL_LEN = 300
GROUPS = 16
CHANS = 75
SIZES = (2, 4, 4, 2)
HELD = 10
ROWS = 80
PITCH = 72
BUNCH = 25

eps = 1e-06


def normalized_templates(library, library_index):
    chosen = lax.dynamic_index_in_dim(library, library_index[0], 0, keepdims=False).astype(jnp.float32)
    centered = chosen - jnp.mean(chosen, axis=-1, keepdims=True)
    factor = lax.rsqrt(jnp.mean(centered * centered, axis=-1, keepdims=True) + eps)
    return (centered * factor).astype(jnp.bfloat16)


def pairs_of(move):
    z_n, y_n, x_n, c_n = SIZES

    def index(z, y, x, c):
        return ((z * y_n + y) * x_n + x) * c_n + c

    pairs = []
    for z in range(z_n):
        for y in range(y_n):
            for x in range(x_n):
                for c in range(c_n):
                    tz, ty, tx, tc = move(z, y, x, c)
                    pairs.append((index(z, y, x, c), index(tz % z_n, ty % y_n, tx % x_n, tc % c_n)))
    return pairs


def spread(block, moves):
    came = [block]
    for move in moves:
        came.append(lax.ppermute(block, "tmpl", pairs_of(move)))
    return came


def join(blocks):
    return jnp.concatenate([block[None] for block in blocks])


def gather_window(window, taps, meta):
    came = lax.ppermute(window, "tmpl", pairs_of(lambda z, y, x, c: (z + 1, y, x, c)))
    fill = ((0, ROWS - CHANS), (0, 0))
    part = join([jnp.pad(window, fill), jnp.pad(came, fill)])
    part = join(spread(part, [lambda z, y, x, c, d=d: (z, y, x + d, c) for d in (1, 2, 3)]))
    part, taps, meta = lax.optimization_barrier((part.reshape(8, ROWS, 128), taps, meta))
    turned = turned_taps(taps)
    early = toeplitz(turned, meta, 0, CHANS - BUNCH)
    late = toeplitz(turned, meta, CHANS - BUNCH, BUNCH)
    part = spread(part, [lambda z, y, x, c, d=d: (z, y + d, x, c) for d in (1, 2, 3)])
    other = []
    for piece in part:
        other.append(lax.ppermute(piece, "tmpl", pairs_of(lambda z, y, x, c: (z, y, x, c + 1))))
    return part + other, early, late, meta


def toeplitz_kernel(origin, count, taps_ref, meta_ref, out_ref):
    def several(step, carry):
        for k in range(BUNCH):
            c = step * BUNCH + k
            base = jnp.broadcast_to(taps_ref[pl.ds(origin + c, 1), :], (8, 512))
            for pair in range(8):
                halves = [
                    pltpu.roll(base, 16 * pair + 8 * h, axis=1, stride=1, stride_axis=0) for h in (0, 1)
                ]
                both = jnp.concatenate(halves, axis=0).astype(jnp.bfloat16)
                for q in range(4):
                    b = -q % 4
                    out_ref[c, 16 * pair : 16 * pair + 16, 128 * q : 128 * q + 128] = both[:, 128 * b : 128 * b + 128]
        return carry

    lax.fori_loop(0, count // BUNCH, several, 0)


def turned_taps(taps):
    row = lax.broadcasted_iota(jnp.int32, (TMPL_LEN, 512), 0)
    column = lax.broadcasted_iota(jnp.int32, (TMPL_LEN, 512), 1)
    return jnp.dot(taps, (((row + column) & 511) == 0).astype(jnp.bfloat16), preferred_element_type=jnp.float32)


def toeplitz(turned, meta, origin, count):
    return pl.pallas_call(
        functools.partial(toeplitz_kernel, origin, count),
        out_shape=jax.ShapeDtypeStruct((count, 128, 512), jnp.bfloat16),
        in_specs=[pl.BlockSpec(memory_space=pltpu.VMEM), pl.BlockSpec(memory_space=pl.ANY)],
        out_specs=pl.BlockSpec(memory_space=pltpu.VMEM),
        compiler_params=pltpu.CompilerParams(vmem_limit_bytes=16 << 20),
        cost_estimate=pl.CostEstimate(flops=count * 65536 * 8, bytes_accessed=count * 131072, transcendentals=0),
    )(turned, meta)


def correlate_kernel(
    meta_ref, m0_ref, m1_ref, m2_ref, m3_ref, n0_ref, n1_ref, n2_ref, n3_ref, early_ref, late_ref,
    o0_ref, o1_ref, o2_ref, o3_ref, rows_ref, inverse_ref, square_ref, shift_ref, acc_ref, band_ref, later_ref,
):
    z0, y0, x0, c0, s0 = (meta_ref[k] for k in range(5))
    acc_ref[...] = jnp.zeros_like(acc_ref)
    band_ref[...] = window_band()
    later_ref[:, 64:, :] = jnp.zeros((3 * BUNCH, PITCH - 64, 128), jnp.float32)
    square_ref[64 * ROWS : 65 * ROWS, :] = jnp.zeros((ROWS, 128), jnp.bfloat16)
    pieces = ((m0_ref, n0_ref), (m1_ref, n1_ref), (m2_ref, n2_ref), (m3_ref, n3_ref))
    for dy, both in enumerate(pieces):
        for dx in range(4):
            for dz in range(2):
                spot = ((((z0 - dz) & 1) * 4 + ((y0 - dy) & 3)) * 4 + ((x0 - dx) & 3)) * 2
                for piece, i in zip(both, (spot + c0, spot + 1 - c0)):
                    block = piece[2 * dx + dz].astype(jnp.float32)
                    rows_ref[pl.ds(i, CHANS, stride=PITCH), :] = block[:CHANS]
                    square_ref[pl.ds(pl.multiple_of(i * ROWS, 16), ROWS), :] = (block * block).astype(jnp.bfloat16)

    carried = jnp.zeros((2 * ROWS, 128), jnp.float32)
    for part in reversed(range(8)):
        squares = jnp.concatenate(
            [square_ref[(8 * part + q) * ROWS : (8 * part + q + 8) * ROWS, :] for q in range(2)], axis=1
        )
        sums = lax.dot_general(
            squares, band_ref[...], (((1,), (0,)), ((), ())), preferred_element_type=jnp.float32
        )
        later = sums[:, 128:]
        total = sums[:, :128] + jnp.concatenate([later[2 * ROWS :], carried], axis=0)
        carried = later[: 2 * ROWS]
        inverse = lax.rsqrt(total * (1.0 / TMPL_LEN) + eps) * (1.0 / TMPL_LEN)
        for k in range(8):
            inverse_ref[pl.ds(8 * part + k, CHANS, stride=PITCH), :] = inverse[k * ROWS : k * ROWS + CHANS]

    lane = lax.broadcasted_iota(jnp.int32, (64, 128), 1)
    line = lax.broadcasted_iota(jnp.int32, (64, 128), 0)

    def bunch(toep_ref, origin, step, carry):
        for k in range(BUNCH):
            c = step * BUNCH + k
            base = pl.multiple_of(c * PITCH, 8)
            parts = lax.dot_general(
                rows_ref[pl.ds(base, 64), :].astype(jnp.bfloat16),
                toep_ref[c - origin],
                (((1,), (0,)), ((), ())),
                preferred_element_type=jnp.float32,
            )
            corr = parts[:, :128]
            for q in (1, 2, 3):
                later_ref[3 * k + q - 1, :64, :] = parts[:, 128 * q : 128 * q + 128]
            for q in (1, 2, 3):
                corr = corr + later_ref[3 * k + q - 1, q : q + 64, :]
            move = meta_ref[5 + c]
            skip, turn = move >> 7, move & 127
            back = (128 - turn) & 127
            shift_ref[k, :64, :] = pltpu.roll(corr * inverse_ref[pl.ds(base, 64), :], back, axis=1)
            moved = jnp.where(
                lane < 128 - turn, shift_ref[k, pl.ds(skip, 64), :], shift_ref[k, pl.ds(skip + 1, 64), :]
            )
            moved = jnp.where(line < 60, moved, 1.0)
            start = pl.multiple_of((meta_ref[5 + CHANS + c] - 2 * s0) * 64, 64)
            acc_ref[pl.ds(start, 64), :] += moved
        return carry

    steps = CHANS // BUNCH - 1
    lax.fori_loop(0, steps, functools.partial(bunch, early_ref, 0), 0)
    bunch(late_ref, steps * BUNCH, steps, 0)
    last = lax.broadcasted_iota(jnp.int32, (8, 128), 0) == 7
    for d, out in enumerate((o0_ref, o1_ref, o2_ref, o3_ref)):
        origin = ((s0 + d) & 3) * 15
        for g in range(HELD):
            upper = acc_ref[pl.ds(64 * g + origin, 8), :]
            lower = acc_ref[pl.ds(64 * g + origin + 8, 8), :]
            lower = jnp.where(last, acc_ref[64 * g + 56 : 64 * g + 64, :], lower)
            out[16 * g : 16 * g + 16, :] = jnp.concatenate([upper, lower], axis=0).astype(jnp.bfloat16)


def combine_kernel(p0_ref, p1_ref, p2_ref, p3_ref, out_ref, sum_ref):
    s0 = lax.axis_index("sta")
    sum_ref[...] = jnp.zeros_like(sum_ref)
    for d, part in enumerate((p0_ref, p1_ref, p2_ref, p3_ref)):
        start = pl.multiple_of(((s0 - d) & 3) * 32, 32)
        sum_ref[pl.ds(start, HELD * 16), :] += part[...].astype(jnp.float32)
    scale = jnp.sqrt(TMPL_LEN / sum_ref[pl.ds(15, GROUPS, stride=16), :])
    for r in range(15):
        rows = sum_ref[pl.ds(r, GROUPS, stride=16), :]
        out_ref[:, 128 * r : 128 * r + 128] = (rows * scale).astype(jnp.bfloat16)


def combine(parts):
    vmem = pl.BlockSpec(memory_space=pltpu.VMEM)
    return pl.pallas_call(
        combine_kernel,
        out_shape=jax.ShapeDtypeStruct((GROUPS, 1920), jnp.bfloat16),
        in_specs=[vmem] * 4,
        out_specs=vmem,
        scratch_shapes=[pltpu.VMEM((256, 128), jnp.float32)],
        compiler_params=pltpu.CompilerParams(vmem_limit_bytes=4 << 20),
    )(*parts)


def correlate(meta, pieces, early, late):
    smem = pl.BlockSpec(memory_space=pltpu.SMEM)
    vmem = pl.BlockSpec(memory_space=pltpu.VMEM)
    return pl.pallas_call(
        correlate_kernel,
        out_shape=[jax.ShapeDtypeStruct((HELD * 16, 128), jnp.bfloat16)] * 4,
        in_specs=[smem] + [vmem] * 10,
        out_specs=[vmem] * 4,
        scratch_shapes=[
            pltpu.VMEM((CHANS * PITCH, 128), jnp.float32),
            pltpu.VMEM((CHANS * PITCH, 128), jnp.float32),
            pltpu.VMEM((65 * ROWS, 128), jnp.bfloat16),
            pltpu.VMEM((BUNCH, PITCH, 128), jnp.float32),
            pltpu.VMEM((HELD * 64, 128), jnp.float32),
            pltpu.VMEM((256, 256), jnp.bfloat16),
            pltpu.VMEM((3 * BUNCH, PITCH, 128), jnp.float32),
        ],
        compiler_params=pltpu.CompilerParams(vmem_limit_bytes=32 << 20),
    )(meta, *pieces, early, late)


def window_band():
    column = lax.broadcasted_iota(jnp.int32, (256, 256), 1)
    late = column >= 128
    row = lax.broadcasted_iota(jnp.int32, (256, 256), 0) + jnp.where(late, 256, 0)
    first = column - jnp.where(late, 128, 0)
    return jnp.where((row >= first) & (row < first + TMPL_LEN), 1.0, 0.0).astype(jnp.bfloat16)


def on_device(window, library, library_index, moveout, group_of):
    me = lax.axis_index("tmpl")
    taps = normalized_templates(library, library_index)
    place = jnp.stack([me >> 5, (me >> 3) & 3, (me >> 1) & 3, me & 1, lax.axis_index("sta")]).astype(jnp.int32)
    meta = jnp.concatenate([place, moveout[0], group_of])
    pieces, early, late, meta = gather_window(window, taps, meta)
    parts = correlate(meta, pieces, early, late)
    came = [parts[0]]
    for d in (1, 2, 3):
        came.append(lax.ppermute(parts[d], "sta", [(i, (i + d) % 4) for i in range(4)]))
    return combine(came)[None]


def solution(mesh):
    in_specs = (P("sta", "tmpl"), P(None, "sta", None), P("tmpl"), P("tmpl", "sta"), P("sta"))
    out_specs = P("tmpl", None, "sta")

    return jax.shard_map(on_device, mesh=mesh, in_specs=in_specs, out_specs=out_specs, check_vma=False)
```
